256 devices in a mesh: row: 32 (over z, x), col: 8 (over y, core).
Axes of the slice: x: 4, y: 4, z: 8, core: 2. Of those that a mesh axis runs over, the one named last changes fastest.
Arguments:
- normal_matrix: float32 [9216, 9216], P('row', 'col'), may hold values from -1 to 6, as said below
- right_side: float32 [9216, 64], P('col'), may hold values from -6 to 6
- tile_inverse: float32 [72, 128, 128], P('col'), may hold values from -1 to 3.5, as said below
- order_ids: int32 [9216], P('col'), may hold values from 0 to 96, never falling along the last dimension, each value on 1 to 194 neighbouring positions
Outputs:
- solution: float32 [9216, 64], P('col')
- residual: float32 [9216, 64], P('col')
The draws below stay inside these ranges and needn't reach their ends.
Inputs may be any that keep to these rules, and one draw needn't show every extreme that they name: `normal_matrix`: symmetric and positive definite. `tile_inverse`: each tile symmetric, every principal submatrix of it positive definite. `order_ids`: never falling along the coefficients; each order holds 1 to 194 coefficients.
All inputs are finite; a program needn't handle non-finite values.
Results may differ from the reference program's by a relative error of at most 0.0003.
Values sent between devices are 32-bit elements; how exact they have to be, the bound alone decides.
No kernel may reach another device: no remote copies, remote signals or barrier semaphores. Data moves between devices by JAX's collectives and lax.ppermute only.
A program may use at most 64 MiB of HBM per device.

```python
import math
import jax
import jax.numpy as jnp
import numpy as np
from jax import lax

NUM = 9216
ORDERS = 97
ORDER_MOST = 194
BLK = 128
NRHS = 64
ITERS = 2


def draw_normal_matrix(key, part):
    first, second = jax.random.split(jax.random.fold_in(key, 11))
    raw = jax.random.normal(first, (NUM, NUM), jnp.float32)
    symmetric = (raw + raw.T) * (0.5 / math.sqrt(NUM))
    diagonal = jax.random.uniform(second, (NUM,), jnp.float32, 2.0, 4.0)
    return symmetric + jnp.diag(diagonal)


def draw_tile_inverse(key, part):
    first, second = jax.random.split(jax.random.fold_in(key, 23))
    raw = jax.random.normal(first, (NUM // BLK, BLK, BLK), jnp.float32)
    symmetric = (raw + jnp.swapaxes(raw, 1, 2)) * (0.3 / math.sqrt(BLK))
    diagonal = jax.random.uniform(second, (NUM // BLK, BLK), jnp.float32, 1.0, 3.0)
    eye = jnp.eye(BLK, dtype=jnp.float32)
    return symmetric + diagonal[:, :, None] * eye[None, :, :]


def block_levels(rng, dims, cuts, least, top_value):
    loudness = 1.0
    for dim, blocks in cuts:
        steps = jax.random.uniform(jax.random.fold_in(jax.random.fold_in(rng, 6), dim), (blocks,), jnp.float32, least / len(cuts), top_value / len(cuts))
        loudness = loudness * jnp.repeat(jnp.exp(steps), dims[dim] // blocks).reshape((-1,) + (1,) * (len(dims) - 1 - dim))
    return loudness


def profile(count, total, limit, lean):
    loads = [(1 << 20) // math.isqrt(standing ** lean) + 1 for standing in range(2, count + 1)]
    surplus, given = total - limit - (count - 1), [1] * (count - 1)
    while surplus > 0:
        free = [i for i in range(count - 1) if given[i] < limit]
        mass, remaining = sum([loads[i] for i in free]), surplus
        for i in free:
            extra = min(limit - given[i], max(1, remaining * loads[i] // mass), surplus)
            given[i] = given[i] + extra
            surplus = surplus - extra
    return np.array([limit] + given)


def ragged(own_key, number_of, total, bound, lean):
    if number_of == 2:
        one = jax.random.randint(own_key, (), max(1, total - bound), min(bound, total - 1) + 1)
        return jnp.stack([one, total - one])
    sizes = jnp.asarray(profile(number_of, total, bound, lean), jnp.int32)
    pairs = (number_of - 1) // 2
    giver, sink = sizes[1:1 + 2 * pairs:2], sizes[2:2 + 2 * pairs:2]
    margin = jnp.minimum(giver - 1, bound - sink)
    passed = jax.random.randint(jax.random.fold_in(own_key, 1), (pairs,), 0, 1 << 20) % (margin + 1)
    sizes = sizes.at[1:1 + 2 * pairs:2].set(giver - passed).at[2:2 + 2 * pairs:2].set(sink + passed)
    return sizes[jax.random.permutation(jax.random.fold_in(own_key, 2), number_of)]


def centred(stream_key, shape, deviation, reach, shards=(), kind=jnp.bfloat16):
    values = deviation * jax.random.normal(stream_key, shape, jnp.float32)
    if shards:
        values = values * block_levels(stream_key, shape, shards, -0.22, 0.18)
    return jnp.clip(values, -reach, reach).astype(kind)


def setup_inputs(seed: int = 0) -> dict:
    keys = jax.random.split(jax.random.key(seed), 5)
    normal_matrix = draw_normal_matrix(jax.random.fold_in(keys[4], 71), 0)
    right_side = centred(keys[1], (NUM, NRHS), 1.0, 6.0, ((0, 8),), jnp.float32)
    tile_inverse = draw_tile_inverse(jax.random.fold_in(keys[4], 71), 0)
    order_ids = jnp.searchsorted(jnp.cumsum(ragged(keys[3], ORDERS, NUM, ORDER_MOST, 0)), jnp.arange(NUM), side="right").astype(jnp.int32)
    return {"normal_matrix": normal_matrix, "right_side": right_side, "tile_inverse": tile_inverse, "order_ids": order_ids}


def apply_precond(tile_inverse, order_ids, vector):
    count = tile_inverse.shape[0]
    width = tile_inverse.shape[1]
    order_tile = order_ids.reshape(count, width)
    same_order = order_tile[:, :, None] == order_tile[:, None, :]
    masked = jnp.where(same_order, tile_inverse, jnp.float32(0.0))
    pieces = vector.reshape(count, width, vector.shape[1])
    result = jnp.einsum("tij,tjk->tik", masked, pieces, precision=lax.Precision.HIGHEST)
    return result.reshape(vector.shape)


def reference(normal_matrix, right_side, tile_inverse, order_ids):
    def apply_matrix(vector):
        return jnp.dot(normal_matrix, vector, precision=lax.Precision.HIGHEST, preferred_element_type=jnp.float32)

    solution = jnp.zeros_like(right_side)
    residual = right_side
    precond_res = apply_precond(tile_inverse, order_ids, residual)
    image_res = apply_matrix(precond_res)
    image_dir = jnp.zeros_like(right_side)
    precond_dir = jnp.zeros_like(right_side)
    residual_dir = jnp.zeros_like(right_side)
    direction = jnp.zeros_like(right_side)
    gamma_prev = jnp.ones((right_side.shape[1],), jnp.float32)
    alpha_prev = jnp.ones((right_side.shape[1],), jnp.float32)
    for iteration in range(ITERS):
        gamma_now = jnp.sum(residual * precond_res, axis=0)
        delta_now = jnp.sum(image_res * precond_res, axis=0)
        precond_img = apply_precond(tile_inverse, order_ids, image_res)
        image_img = apply_matrix(precond_img)
        if iteration == 0:
            beta_ratio = jnp.zeros_like(gamma_now)
            step_size = gamma_now / delta_now
        else:
            beta_ratio = gamma_now / gamma_prev
            step_size = gamma_now / (delta_now - beta_ratio * gamma_now / alpha_prev)
        image_dir = image_img + beta_ratio * image_dir
        precond_dir = precond_img + beta_ratio * precond_dir
        residual_dir = image_res + beta_ratio * residual_dir
        direction = precond_res + beta_ratio * direction
        solution = solution + step_size * direction
        residual = residual - step_size * residual_dir
        precond_res = precond_res - step_size * precond_dir
        image_res = image_res - step_size * image_dir
        gamma_prev = gamma_now
        alpha_prev = step_size
    return solution, residual
```

```python
import jax
import jax.numpy as jnp
from jax import lax
from jax.experimental import pallas as pl
from jax.experimental.pallas import tpu as pltpu
from jax.sharding import PartitionSpec as P


HIGHEST = lax.Precision.HIGHEST
BOTH = ("row", "col")
Z, X, Y, K = 8, 4, 4, 2
TILE = 128
PART = 18


def place(z, x, y, k):
    return ((z % Z) * X + x % X) * (Y * K) + (y % Y) * K + k % K


def everyone():
    return [(z, x, y, k) for z in range(Z) for x in range(X) for y in range(Y) for k in range(K)]


def moved(array, to):
    pairs = [(place(*at), place(*to(*at))) for at in everyone()]
    return lax.ppermute(array, BOTH, pairs)


def moved_from(array, holders, to):
    pairs = [(place(*at), place(*to(*at))) for at in everyone() if holders(*at)]
    return lax.ppermute(array, BOTH, pairs)


def other_core(array):
    return moved(array, lambda z, x, y, k: (z, x, y, k + 1))


def around_y(array):
    return [moved(array, lambda z, x, y, k: (z, x, y + step, k)) for step in (1, 3, 2)]


def dot(a, b):
    return jnp.dot(a, b, precision=HIGHEST, preferred_element_type=jnp.float32)


def masked_kernel(right_ref, tile_ref, order_ref, precond_ref, masked_ref):
    for t in range(tile_ref.shape[0]):
        rows = pl.ds(t * TILE, TILE)
        across = jnp.broadcast_to(order_ref[t : t + 1, :], (TILE, TILE)).astype(jnp.float32)
        masked = jnp.where(across == across.T, tile_ref[t], 0.0)
        masked_ref[t] = masked
        precond_ref[rows, :] = dot(masked, right_ref[rows, :])


def middle_kernel(shift_ref, own_ref, one_ref, two_ref, three_ref, held_ref, last_ref, image_ref, total_ref, window, spread):
    shift = pl.multiple_of(shift_ref[0], 8)
    total = own_ref[...] + one_ref[...] + two_ref[...] + three_ref[...]
    total_ref[...] = total
    half = total.shape[0]
    wide = total.shape[1] // 2
    window[...] = jnp.zeros_like(window)
    window[pl.ds(shift, half), :] = total[:, :wide]
    window[pl.ds(shift + half, half), :] = total[:, wide:]
    spread[...] = jnp.zeros_like(spread)
    edge = 96
    for t in range(3):
        rows = pl.ds(t * TILE, TILE)
        tile = held_ref[rows, :] + last_ref[rows, :]
        spread[pl.ds(edge + t * TILE, TILE), :] = dot(tile, window[rows, :])
    image_ref[...] = spread[pl.ds(shift, image_ref.shape[0]), :]


def gathered_kernel(all_ref, right_ref, precond_ref, masked_ref, image_ref, second_ref, third_ref, dots_ref):
    wide = right_ref.shape[1]
    half = PART * Z
    for x in range(X):
        for k in range(Z):
            part = all_ref[k * X + x, PART : 2 * PART, :]
            image_ref[pl.ds(2 * half * x + PART * k, PART), :] = part[:, :wide]
            image_ref[pl.ds(2 * half * x + half + PART * k, PART), :] = part[:, wide:]
    count = masked_ref.shape[0]
    sums = [jnp.zeros((8, wide), jnp.float32) for _ in range(6)]
    for t in range(count):
        rows = pl.ds(t * TILE, TILE)
        flat = jnp.concatenate([all_ref[:, t, :], all_ref[:, count + t, :]], axis=0)
        third = flat.T
        third_ref[rows, :] = third
        image = image_ref[rows, :]
        second = dot(masked_ref[t], image)
        second_ref[rows, :] = second
        right, precond = right_ref[rows, :], precond_ref[rows, :]
        pairs = ((right, precond), (image, precond), (right, second), (image, second), (third, precond), (third, second))
        for i, (a, b) in enumerate(pairs):
            sums[i] = sums[i] + jnp.sum((a * b).reshape(TILE // 8, 8, wide), axis=0)
    lines = [jnp.sum(s, axis=0, keepdims=True) for s in sums]
    dots_ref[...] = jnp.concatenate(lines + [lines[0], lines[0]], axis=0)


def last_kernel(a_ref, b_ref, c_ref, d_ref, right_ref, precond_ref, image_ref, second_ref, third_ref, solution_ref, residual_ref):
    dots = a_ref[...] + b_ref[...] + c_ref[...] + d_ref[...]
    gamma, delta, rm, wm, nu, nm = [dots[i : i + 1, :] for i in range(6)]
    alpha = gamma / delta
    gamma_next = gamma - alpha * (delta + rm) + alpha * alpha * wm
    delta_next = delta - alpha * (nu + wm) + alpha * alpha * nm
    beta = gamma_next / gamma
    step = gamma_next / (delta_next - beta * gamma_next / alpha)
    u, w = precond_ref[...], image_ref[...]
    u_next = u - alpha * second_ref[...]
    w_next = w - alpha * third_ref[...]
    solution_ref[...] = alpha * u + step * (u_next + beta * u)
    residual_ref[...] = (right_ref[...] - alpha * w) - step * (w_next + beta * w)


def shaped(*dims):
    return jax.ShapeDtypeStruct(dims, jnp.float32)


def body(normal_matrix, right_side, tile_inverse, order_ids):
    block_rows, block_cols = normal_matrix.shape
    wide = right_side.shape[1]
    count = tile_inverse.shape[0]
    half = block_rows // 2
    edge = 96
    row = lax.axis_index("row")
    col = lax.axis_index("col")
    x = row % X
    root = col == row // X

    before = moved(normal_matrix[block_rows - edge :], lambda z, x, y, k: (z, x + 1, y, k))
    after = moved(normal_matrix[:edge], lambda z, x, y, k: (z, x - 1, y, k))

    precond_res, masked = pl.pallas_call(
        masked_kernel,
        out_shape=(shaped(count * TILE, wide), shaped(count, TILE, TILE)),
    )(right_side, tile_inverse, order_ids.reshape(count, TILE))

    three = lax.dynamic_slice_in_dim(masked, 2 * x, 3, 0).reshape(3 * TILE, TILE)
    held = jnp.where(root, three, 0.0)
    held = held + moved_from(held, lambda z, x, y, k: (y, k) == (z // 2, z % 2), lambda z, x, y, k: (z, x, y, k + 1))
    held = held + moved_from(held, lambda z, x, y, k: y == z // 2, lambda z, x, y, k: (z, x, y ^ 1, k))
    last = moved_from(held, lambda z, x, y, k: y // 2 == z // 4, lambda z, x, y, k: (z, x, y ^ 2, k))

    partial_value = dot(normal_matrix, precond_res)
    packed = jnp.concatenate([partial_value[:half], partial_value[half:]], axis=1)
    packed = packed + other_core(packed)
    image_ext, image_res = pl.pallas_call(
        middle_kernel,
        out_shape=(shaped(block_rows + 2 * edge, wide), shaped(half, 2 * wide)),
        in_specs=[pl.BlockSpec(memory_space=pltpu.SMEM)] + [pl.BlockSpec(memory_space=pltpu.VMEM)] * 6,
        scratch_shapes=[pltpu.VMEM((3 * TILE, wide), jnp.float32), pltpu.VMEM((3 * TILE + 2 * edge, wide), jnp.float32)],
    )((32 * x).astype(jnp.int32).reshape(1), packed, *around_y(packed), held, last)

    part = lax.dynamic_slice_in_dim(image_res, PART * col, PART, 0)
    part = moved(part, lambda z, x, y, k: (y * K + k, x, z // 2, z % 2))

    matrix_ext = jnp.concatenate([before, normal_matrix, after], axis=0)
    second_flat = lax.dot_general(image_ext, matrix_ext, (((0,), (0,)), ((), ())), precision=HIGHEST, preferred_element_type=jnp.float32)
    pieces = second_flat.reshape(2, Z * X, block_cols).swapaxes(0, 1)
    pieces = lax.all_to_all(pieces, "row", 0, 0, tiled=True)
    own = jnp.sum(pieces, axis=0).reshape(PART, 2 * wide)

    payload = jnp.concatenate([own, part], axis=0)
    copies = jnp.broadcast_to(payload, (Z * X, *payload.shape))
    whole = lax.all_to_all(copies, "row", 0, 0, tiled=True)

    image, second, third, dots = pl.pallas_call(
        gathered_kernel,
        out_shape=(shaped(block_cols, wide), shaped(block_cols, wide), shaped(block_cols, wide), shaped(8, wide)),
    )(whole, right_side, precond_res, masked)

    dots = dots + other_core(dots)
    return pl.pallas_call(
        last_kernel,
        out_shape=(shaped(block_cols, wide), shaped(block_cols, wide)),
    )(dots, *around_y(dots), right_side, precond_res, image, second, third)


def solution(mesh):
    return jax.shard_map(
        body,
        mesh=mesh,
        in_specs=(P("row", "col"), P("col", None), P("col", None, None), P("col")),
        out_specs=(P("col", None), P("col", None)),
        check_vma=False,
    )
```

```python
import jax
import jax.numpy as jnp
from jax import lax
from jax.experimental import pallas as pl
from jax.experimental.pallas import tpu as pltpu
from jax.sharding import PartitionSpec as P


HIGHEST = lax.Precision.HIGHEST
BOTH = ("row", "col")
Z, X, Y, K = 8, 4, 4, 2
COLS = Y * K
TILE = 128
PART = 18
STEPS = (0, 1, -1, 2, -2, 3, -3, 4)


def place(z, x, y, k):
    return ((z % Z) * X + x % X) * COLS + (y % Y) * K + k % K


def everyone():
    return [(z, x, y, k) for z in range(Z) for x in range(X) for y in range(Y) for k in range(K)]


def moved(array, to):
    pairs = [(place(*at), place(*to(*at))) for at in everyone()]
    return lax.ppermute(array, BOTH, pairs)


def other_core(array):
    return moved(array, lambda z, x, y, k: (z, x, y, k + 1))


def step_y(array, step):
    return moved(array, lambda z, x, y, k: (z, x, y + step, k))


def hop_order(plane):
    def away(piece):
        gap = (piece // K - plane // K) % Y
        return min(gap, Y - gap)

    return sorted(range(COLS), key=lambda piece: (-away(piece), piece))


def into_column(array):
    def to(z, x, y, k):
        return (z + STEPS[hop_order(z).index(y * K + k)], x, z // K, z % K)

    return moved(array, to)


SOURCES = [[(plane + STEPS[hop_order(plane).index(piece)]) % Z for piece in range(COLS)] for plane in range(COLS)]


def dot(a, b):
    return jnp.dot(a, b, precision=HIGHEST, preferred_element_type=jnp.float32)


def put_pieces(value, pieces, spot_ref, keep_ref, send_ref, line=None):
    for p in range(COLS):
        low = value[2 * PART * p : 2 * PART * p + PART]
        high = value[2 * PART * p + PART : 2 * PART * (p + 1)]
        pieces[p, 0:PART, :] = jnp.concatenate([low, high], axis=1)
    y, k = spot_ref[0], spot_ref[1]
    for j in range(Y):
        at = lax.rem(y + j, Y) * K
        keep_ref[j, 0:PART, :] = pieces[at + k, 0:PART, :]
        send_ref[j, 0:PART, :] = pieces[at + 1 - k, 0:PART, :]
        if line is not None:
            tail = keep_ref.shape[1] - PART
            keep_ref[j, PART:, :] = jnp.broadcast_to(line, (tail, line.shape[1]))
            send_ref[j, PART:, :] = jnp.broadcast_to(line, (tail, line.shape[1]))


def take_pieces(all_ref, spot_ref, out_ref):
    wide = out_ref.shape[1]
    for p in range(COLS):
        z = spot_ref[2 + p]
        for x in range(X):
            part = all_ref[z * X + x]
            at = 2 * PART * (COLS * x + p)
            out_ref[pl.ds(at, PART), :] = part[:, :wide]
            out_ref[pl.ds(at + PART, PART), :] = part[:, wide:]


def summed(a):
    return jnp.sum(a, axis=0, keepdims=True)


def first_kernel(spot_ref, flat_ref, tile_ref, order_ref, matrix_hbm, keep_ref, send_ref, right_ref, precond_ref, masked_ref, matrix, pieces, sem):
    copy = pltpu.make_async_copy(matrix_hbm, matrix, sem)
    copy.start()
    for t in range(tile_ref.shape[0]):
        rows = pl.ds(t * TILE, TILE)
        across = jnp.broadcast_to(order_ref[t : t + 1, :], (TILE, TILE)).astype(jnp.float32)
        masked = jnp.where(across == across.T, tile_ref[t], 0.0)
        masked_ref[t] = masked
        right = flat_ref[:, rows].T
        right_ref[rows, :] = right
        precond_ref[rows, :] = dot(masked, right)
    copy.wait()
    put_pieces(dot(matrix[...], precond_ref[...]), pieces, spot_ref, keep_ref, send_ref)


def second_kernel(spot_ref, all_ref, right_ref, precond_ref, masked_ref, matrix_hbm, keep_ref, send_ref, image_ref, second_ref, matrix, pieces, sem):
    copy = pltpu.make_async_copy(matrix_hbm, matrix, sem)
    copy.start()
    take_pieces(all_ref, spot_ref, image_ref)
    for t in range(masked_ref.shape[0]):
        rows = pl.ds(t * TILE, TILE)
        second_ref[rows, :] = dot(masked_ref[t], image_ref[rows, :])
    precond = precond_ref[...]
    gamma = summed(right_ref[...] * precond)
    delta = summed(image_ref[...] * precond)
    line = jnp.concatenate([gamma, delta], axis=1)
    copy.wait()
    put_pieces(dot(matrix[...], second_ref[...]), pieces, spot_ref, keep_ref, send_ref, line)


def third_kernel(spot_ref, all_ref, sums_ref, right_ref, precond_ref, image_ref, second_ref, third_ref, dots_ref):
    wide = right_ref.shape[1]
    take_pieces(all_ref, spot_ref, third_ref)
    gamma, delta = sums_ref[PART : PART + 1, :wide], sums_ref[PART : PART + 1, wide:]
    alpha = gamma / delta
    precond = precond_ref[...] - alpha * second_ref[...]
    gamma_next = summed((right_ref[...] - alpha * image_ref[...]) * precond)
    delta_next = summed((image_ref[...] - alpha * third_ref[...]) * precond)
    line = jnp.concatenate([gamma_next, delta_next], axis=1)
    dots_ref[...] = jnp.broadcast_to(line, dots_ref.shape)


def last_kernel(a_ref, b_ref, c_ref, d_ref, sums_ref, right_ref, precond_ref, image_ref, second_ref, third_ref, solution_ref, residual_ref):
    wide = right_ref.shape[1]
    gamma, delta = sums_ref[PART : PART + 1, :wide], sums_ref[PART : PART + 1, wide:]
    alpha = gamma / delta
    dots = (a_ref[...] + b_ref[...] + c_ref[...] + d_ref[...])[0:1]
    gamma_next, delta_next = dots[:, :wide], dots[:, wide:]
    beta = gamma_next / gamma
    step = gamma_next / (delta_next - beta * gamma_next / alpha)
    for t in range(right_ref.shape[0] // TILE):
        rows = pl.ds(t * TILE, TILE)
        u, w = precond_ref[rows, :], image_ref[rows, :]
        u_next = u - alpha * second_ref[rows, :]
        w_next = w - alpha * third_ref[rows, :]
        solution_ref[:, rows] = (alpha * u + step * (u_next + beta * u)).T
        residual_ref[:, rows] = ((right_ref[rows, :] - alpha * w) - step * (w_next + beta * w)).T


def shaped(*dims):
    return jax.ShapeDtypeStruct(dims, jnp.float32)


SMEM = pl.BlockSpec(memory_space=pltpu.SMEM)
VMEM = pl.BlockSpec(memory_space=pltpu.VMEM)
ANY = pl.BlockSpec(memory_space=pl.ANY)


def spread_out(keep, send):
    both = keep + other_core(send)
    parts = [step_y(both[j], j) for j in (1, 3, 2)]
    sums = both[0] + parts[0] + parts[1] + parts[2]
    chunk = into_column(sums[:PART])
    copies = jnp.broadcast_to(chunk, (Z * X, *chunk.shape))
    return sums, lax.all_to_all(copies, "row", 0, 0, tiled=True)


def body(normal_matrix, right_side, tile_inverse, order_ids):
    block_rows, block_cols = normal_matrix.shape
    wide = right_side.shape[1]
    count = tile_inverse.shape[0]
    col = lax.axis_index("col")
    spot = jnp.concatenate([jnp.stack([col // K, col % K]).astype(jnp.int32), jnp.asarray(SOURCES, jnp.int32)[col]])
    vector = shaped(block_cols, wide)
    scratch = [
        pltpu.VMEM((block_rows, block_cols), jnp.float32),
        pltpu.VMEM((COLS, 24, 2 * wide), jnp.float32),
        pltpu.SemaphoreType.DMA(()),
    ]

    keep, send, right, precond, masked = pl.pallas_call(
        first_kernel,
        out_shape=(shaped(Y, PART, 2 * wide), shaped(Y, PART, 2 * wide), vector, vector, shaped(count, TILE, TILE)),
        in_specs=[SMEM, VMEM, VMEM, VMEM, ANY],
        scratch_shapes=scratch,
    )(spot, right_side.T, tile_inverse, order_ids.reshape(count, TILE), normal_matrix)
    _, whole = spread_out(keep, send)

    lines = PART + 2
    keep, send, image, second = pl.pallas_call(
        second_kernel,
        out_shape=(shaped(Y, lines, 2 * wide), shaped(Y, lines, 2 * wide), vector, vector),
        in_specs=[SMEM, VMEM, VMEM, VMEM, VMEM, ANY],
        scratch_shapes=scratch,
    )(spot, whole, right, precond, masked, normal_matrix)
    sums, whole = spread_out(keep, send)

    third, dots = pl.pallas_call(
        third_kernel,
        out_shape=(vector, shaped(8, 2 * wide)),
        in_specs=[SMEM] + [VMEM] * 6,
    )(spot, whole, sums, right, precond, image, second)

    dots = dots + other_core(dots)
    flat = shaped(wide, block_cols)
    solution, residual = pl.pallas_call(last_kernel, out_shape=(flat, flat))(
        dots, step_y(dots, 1), step_y(dots, 3), step_y(dots, 2), sums, right, precond, image, second, third
    )
    return solution.T, residual.T


def solution(mesh):
    return jax.shard_map(
        body,
        mesh=mesh,
        in_specs=(P("row", "col"), P("col", None), P("col", None, None), P("col")),
        out_specs=(P("col", None), P("col", None)),
        check_vma=False,
    )
```

```python
import jax
import jax.numpy as jnp
from jax import lax
from jax.experimental import pallas as pl
from jax.experimental.pallas import tpu as pltpu
from jax.sharding import PartitionSpec as P


BOTH = ("row", "col")
Z, X, Y, K = 8, 4, 4, 2
COLS = Y * K
TILE = 128
PART = 18
REACH = (3, 1, 0, 2)


def place(z, x, y, k):
    return ((z % Z) * X + x % X) * COLS + (y % Y) * K + k % K


def everyone():
    return [(z, x, y, k) for z in range(Z) for x in range(X) for y in range(Y) for k in range(K)]


def moved(array, to):
    pairs = [(place(*at), place(*to(*at))) for at in everyone()]
    return lax.ppermute(array, BOTH, pairs)


def other_core(array):
    return moved(array, lambda z, x, y, k: (z, x, y, k + 1))


def step_y(array, step):
    return moved(array, lambda z, x, y, k: (z, x, y + step, k))


def hop(plane, y, k):
    reach = REACH[(y - plane // K) % Y]
    return 1 + reach if k else -reach


def into_column(array):
    return moved(array, lambda z, x, y, k: (z + hop(z, y, k), x, z // K, z % K))


def parts_of(a):
    top = a.astype(jnp.bfloat16)
    rest = a - top.astype(jnp.float32)
    mid = rest.astype(jnp.bfloat16)
    return top, mid, (rest - mid.astype(jnp.float32)).astype(jnp.bfloat16)


def pass_of(a, b):
    return jnp.dot(a, b, preferred_element_type=jnp.float32)


def product(left_parts, right):
    n = right.shape[1]
    top, mid, low = left_parts
    side = jnp.concatenate(parts_of(right), axis=1)
    one = pass_of(top, side)
    two = pass_of(mid, side[:, : 2 * n])
    three = pass_of(low, side[:, :n])
    return one[:, :n] + ((one[:, n : 2 * n] + two[:, :n]) + ((one[:, 2 * n :] + two[:, n:]) + three))


def put_pieces(value, pieces, spot_ref, keep_ref, send_ref, line=None):
    for p in range(COLS):
        low = value[2 * PART * p : 2 * PART * p + PART]
        high = value[2 * PART * p + PART : 2 * PART * (p + 1)]
        pieces[p, 0:PART, :] = jnp.concatenate([low, high], axis=1)
    y, k = lax.div(spot_ref[0], K), lax.rem(spot_ref[0], K)
    for j in range(Y):
        at = lax.rem(y + j, Y) * K
        keep_ref[j, 0:PART, :] = pieces[at + k, 0:PART, :]
        send_ref[j, 0:PART, :] = pieces[at + 1 - k, 0:PART, :]
        if line is not None:
            tail = keep_ref.shape[1] - PART
            keep_ref[j, PART:, :] = jnp.broadcast_to(line, (tail, line.shape[1]))
            send_ref[j, PART:, :] = jnp.broadcast_to(line, (tail, line.shape[1]))


def take_pieces(all_ref, spot_ref, out_ref):
    wide = out_ref.shape[1]
    col = spot_ref[0]
    for p in range(COLS):
        turn = lax.rem(p // K + Y - lax.div(col, K), Y)
        reach = jnp.where(turn == 0, REACH[0], jnp.where(turn == 1, REACH[1], jnp.where(turn == 2, REACH[2], REACH[3])))
        z = lax.rem(col + (1 + reach if p % K else Z - reach), Z)
        for x in range(X):
            part = all_ref[z * X + x]
            at = 2 * PART * (COLS * x + p)
            out_ref[pl.ds(at, PART), :] = part[:, :wide]
            out_ref[pl.ds(at + PART, PART), :] = part[:, wide:]


def summed(a):
    return jnp.sum(a, axis=0, keepdims=True)


def first_kernel(spot_ref, flat_ref, tile_ref, order_ref, matrix_hbm, keep_ref, send_ref, right_ref, precond_ref, masked_ref, matrix, pieces, sem):
    copy = pltpu.make_async_copy(matrix_hbm, matrix, sem)
    copy.start()
    for t in range(tile_ref.shape[0]):
        rows = pl.ds(t * TILE, TILE)
        across = jnp.broadcast_to(order_ref[t : t + 1, :], (TILE, TILE)).astype(jnp.float32)
        masked = jnp.where(across == across.T, tile_ref[t], 0.0)
        masked_ref[t] = masked
        right = flat_ref[:, rows].T
        right_ref[rows, :] = right
        precond_ref[rows, :] = product(parts_of(masked), right)
    copy.wait()
    put_pieces(product(parts_of(matrix[...]), precond_ref[...]), pieces, spot_ref, keep_ref, send_ref)


def second_kernel(spot_ref, all_ref, right_ref, precond_ref, masked_ref, matrix_hbm, keep_ref, send_ref, image_ref, second_ref, matrix, pieces, sem):
    copy = pltpu.make_async_copy(matrix_hbm, matrix, sem)
    copy.start()
    take_pieces(all_ref, spot_ref, image_ref)
    for t in range(masked_ref.shape[0]):
        rows = pl.ds(t * TILE, TILE)
        second_ref[rows, :] = product(parts_of(masked_ref[t]), image_ref[rows, :])
    precond = precond_ref[...]
    gamma = summed(right_ref[...] * precond)
    delta = summed(image_ref[...] * precond)
    line = jnp.concatenate([gamma, delta], axis=1)
    copy.wait()
    put_pieces(product(parts_of(matrix[...]), second_ref[...]), pieces, spot_ref, keep_ref, send_ref, line)


def third_kernel(spot_ref, all_ref, sums_ref, right_ref, precond_ref, image_ref, second_ref, third_ref, dots_ref):
    wide = right_ref.shape[1]
    take_pieces(all_ref, spot_ref, third_ref)
    gamma, delta = sums_ref[PART : PART + 1, :wide], sums_ref[PART : PART + 1, wide:]
    alpha = gamma / delta
    precond = precond_ref[...] - alpha * second_ref[...]
    gamma_next = summed((right_ref[...] - alpha * image_ref[...]) * precond)
    delta_next = summed((image_ref[...] - alpha * third_ref[...]) * precond)
    line = jnp.concatenate([gamma_next, delta_next], axis=1)
    dots_ref[...] = jnp.broadcast_to(line, dots_ref.shape)


def last_kernel(a_ref, b_ref, c_ref, d_ref, sums_ref, right_ref, precond_ref, image_ref, second_ref, third_ref, solution_ref, residual_ref):
    wide = right_ref.shape[1]
    gamma, delta = sums_ref[PART : PART + 1, :wide], sums_ref[PART : PART + 1, wide:]
    alpha = gamma / delta
    dots = (a_ref[...] + b_ref[...] + c_ref[...] + d_ref[...])[0:1]
    gamma_next, delta_next = dots[:, :wide], dots[:, wide:]
    beta = gamma_next / gamma
    step = gamma_next / (delta_next - beta * gamma_next / alpha)
    for t in range(right_ref.shape[0] // TILE):
        rows = pl.ds(t * TILE, TILE)
        u, w = precond_ref[rows, :], image_ref[rows, :]
        u_next = u - alpha * second_ref[rows, :]
        w_next = w - alpha * third_ref[rows, :]
        solution_ref[:, rows] = (alpha * u + step * (u_next + beta * u)).T
        residual_ref[:, rows] = ((right_ref[rows, :] - alpha * w) - step * (w_next + beta * w)).T


def shaped(*dims):
    return pltpu.VMEM(dims, jnp.float32)


def near(*arrays):
    return [pltpu.with_memory_space_constraint(a, pltpu.VMEM) for a in arrays]


SMEM = pl.BlockSpec(memory_space=pltpu.SMEM)
VMEM = pl.BlockSpec(memory_space=pltpu.VMEM)
ANY = pl.BlockSpec(memory_space=pl.ANY)


def spread_out(keep, send):
    both = keep + other_core(send)
    parts = [step_y(both[j], j) for j in (1, 3, 2)]
    sums = both[0] + parts[0] + parts[1] + parts[2]
    chunk = into_column(sums[:PART])
    copies = jnp.broadcast_to(chunk, (Z * X, *chunk.shape))
    return sums, lax.all_to_all(copies, "row", 0, 0, tiled=True)


def body(normal_matrix, right_side, tile_inverse, order_ids):
    block_rows, block_cols = normal_matrix.shape
    wide = right_side.shape[1]
    count = tile_inverse.shape[0]
    spot = lax.axis_index("col").astype(jnp.int32).reshape(1)
    vector = shaped(block_cols, wide)
    scratch = [
        pltpu.VMEM((block_rows, block_cols), jnp.float32),
        pltpu.VMEM((COLS, 24, 2 * wide), jnp.float32),
        pltpu.SemaphoreType.DMA(()),
    ]

    keep, send, right, precond, masked = pl.pallas_call(
        first_kernel,
        out_shape=(shaped(Y, PART, 2 * wide), shaped(Y, PART, 2 * wide), vector, vector, shaped(count, TILE, TILE)),
        in_specs=[SMEM, VMEM, VMEM, VMEM, ANY],
        scratch_shapes=scratch,
    )(spot, right_side.T, tile_inverse, order_ids.reshape(count, TILE), normal_matrix)
    _, whole = spread_out(keep, send)

    lines = PART + 2
    keep, send, image, second = pl.pallas_call(
        second_kernel,
        out_shape=(shaped(Y, lines, 2 * wide), shaped(Y, lines, 2 * wide), vector, vector),
        in_specs=[SMEM, VMEM, VMEM, VMEM, VMEM, ANY],
        scratch_shapes=scratch,
    )(spot, *near(whole, right, precond, masked), normal_matrix)
    sums, whole = spread_out(keep, send)

    third, dots = pl.pallas_call(
        third_kernel,
        out_shape=(vector, shaped(8, 2 * wide)),
        in_specs=[SMEM] + [VMEM] * 6,
    )(spot, *near(whole, sums, right, precond, image, second))

    dots = dots + other_core(dots)
    flat = jax.ShapeDtypeStruct((wide, block_cols), jnp.float32)
    solution, residual = pl.pallas_call(last_kernel, out_shape=(flat, flat), in_specs=[VMEM] * 10)(
        *near(dots, step_y(dots, 1), step_y(dots, 3), step_y(dots, 2), sums, right, precond, image, second, third)
    )
    return solution.T, residual.T


def solution(mesh):
    return jax.shard_map(
        body,
        mesh=mesh,
        in_specs=(P("row", "col"), P("col", None), P("col", None, None), P("col")),
        out_specs=(P("col", None), P("col", None)),
        check_vma=False,
    )
```

```python
import jax
import jax.numpy as jnp
from jax import lax
from jax.experimental import pallas as pl
from jax.experimental.pallas import tpu as pltpu
from jax.sharding import PartitionSpec as P


BOTH = ("row", "col")
Z, X, Y, K = 8, 4, 4, 2
COLS = Y * K
TILE = 128
HALF = 144
LINES = 8
REACH = (3, 1, 0, 2)
STEPS = (1, 3, 2)


def place(z, x, y, k):
    return ((z % Z) * X + x % X) * COLS + (y % Y) * K + k % K


def everyone():
    return [(z, x, y, k) for z in range(Z) for x in range(X) for y in range(Y) for k in range(K)]


def moved(array, to):
    pairs = [(place(*at), place(*to(*at))) for at in everyone()]
    return lax.ppermute(array, BOTH, pairs)


def other_core(array):
    return moved(array, lambda z, x, y, k: (z, x, y, k + 1))


def step_y(array, step):
    return moved(array, lambda z, x, y, k: (z, x, y + step, k))


def step_x(array, step):
    return moved(array, lambda z, x, y, k: (z, x + step, y, k))


def hop(plane, y, k):
    reach = REACH[(y - plane // K) % Y]
    return 1 + reach if k else -reach


def into_column(array):
    return moved(array, lambda z, x, y, k: (z + hop(z, y, k), x, z // K, z % K))


def parts_of(a):
    top = a.astype(jnp.bfloat16)
    rest = a - top.astype(jnp.float32)
    mid = rest.astype(jnp.bfloat16)
    return top, mid, (rest - mid.astype(jnp.float32)).astype(jnp.bfloat16)


def pass_of(a, b):
    return jnp.dot(a, b, preferred_element_type=jnp.float32)


def product(left, right):
    n = right.shape[1]
    top, mid, low = parts_of(left)
    side = jnp.concatenate(parts_of(right), axis=1)
    one = pass_of(top, side)
    two = pass_of(mid, side[:, : 2 * n])
    three = pass_of(low, side[:, :n])
    return one[:, :n] + ((one[:, n : 2 * n] + two[:, :n]) + ((one[:, 2 * n :] + two[:, n:]) + three))


def summed(a):
    return jnp.sum(a, axis=0, keepdims=True)


def put_rows(value, line, packed_ref):
    packed_ref[0:HALF, :] = jnp.concatenate([value[:HALF], value[HALF:]], axis=1)
    packed_ref[HALF:, :] = jnp.broadcast_to(line, (LINES, line.shape[1]))


def take_rows(x, block_refs, out_ref):
    wide = out_ref.shape[1]
    for step, ref in zip((0,) + STEPS, block_refs):
        at = pl.multiple_of(lax.rem(x + X - step, X) * (2 * HALF), 8)
        block = ref[0:HALF, :]
        out_ref[pl.ds(at, HALF), :] = block[:, :wide]
        out_ref[pl.ds(at + HALF, HALF), :] = block[:, wide:]


def copies_of(sources, targets, sems):
    return [pltpu.make_async_copy(s, t, sems.at[i]) for i, (s, t) in enumerate(zip(sources, targets))]


def thirds(ref):
    return [ref.at[pl.ds(3 * i, 3)] for i in range(ref.shape[0] // 3)]


def first_kernel(order_ref, flat_hbm, tile_hbm, matrix_hbm, packed_ref, right_hbm, precond_hbm, masked_hbm, flat, tiles, matrix, right, precond, masked, in_sems, out_sems):
    arrivals = copies_of([flat_hbm, *thirds(tile_hbm), matrix_hbm], [flat, *thirds(tiles), matrix], in_sems)
    for copy in arrivals:
        copy.start()
    eye = lax.broadcasted_iota(jnp.int32, (TILE, TILE), 0) == lax.broadcasted_iota(jnp.int32, (TILE, TILE), 1)
    ones = jnp.ones((TILE, TILE), jnp.bfloat16)
    arrivals[0].wait()
    wide = flat.shape[0]
    gamma = jnp.zeros((1, wide), jnp.float32)
    for t in range(tiles.shape[0]):
        if t % 3 == 0:
            arrivals[1 + t // 3].wait()
        rows = pl.ds(t * TILE, TILE)
        across = jnp.broadcast_to(order_ref[t : t + 1, :].astype(jnp.float32), (TILE, TILE))
        down = pass_of(jnp.where(eye, across, 0.0).astype(jnp.bfloat16), ones)
        tile = jnp.where(across == down, tiles[t], 0.0)
        masked[t] = tile
        side = flat[:, rows].T
        right[rows, :] = side
        own = product(tile, side)
        precond[rows, :] = own
        gamma = gamma + summed(side * own)
    leaving = copies_of([right, precond, masked], [right_hbm, precond_hbm, masked_hbm], out_sems)
    for copy in leaving:
        copy.start()
    arrivals[-1].wait()
    put_rows(product(matrix[...], precond[...]), jnp.concatenate([gamma, jnp.zeros_like(gamma)], axis=1), packed_ref)
    for copy in leaving:
        copy.wait()


def second_kernel(spot_ref, a_ref, b_ref, c_ref, d_ref, precond_hbm, masked_hbm, matrix_hbm, packed_ref, image_hbm, second_hbm, precond, masked, matrix, image, second, in_sems, out_sems):
    arrivals = copies_of([*thirds(masked_hbm), matrix_hbm, precond_hbm], [*thirds(masked), matrix, precond], in_sems)
    for copy in arrivals:
        copy.start()
    wide = image.shape[1]
    leaving = copies_of([image, second], [image_hbm, second_hbm], out_sems)
    take_rows(spot_ref[0], (a_ref, b_ref, c_ref, d_ref), image)
    leaving[0].start()
    for t in range(masked.shape[0]):
        if t % 3 == 0:
            arrivals[t // 3].wait()
        rows = pl.ds(t * TILE, TILE)
        second[rows, :] = product(masked[t], image[rows, :])
    leaving[1].start()
    arrivals[-1].wait()
    delta = summed(image[...] * precond[...])
    gamma = jnp.where(spot_ref[1] == 0, a_ref[HALF : HALF + 1, :wide], 0.0)
    arrivals[-2].wait()
    put_rows(product(matrix[...], second[...]), jnp.concatenate([gamma, delta], axis=1), packed_ref)
    for copy in leaving:
        copy.wait()


def third_kernel(spot_ref, a_ref, b_ref, c_ref, d_ref, right_ref, precond_ref, image_ref, second_ref, dots_ref, third):
    wide = right_ref.shape[1]
    take_rows(spot_ref[0], (a_ref, b_ref, c_ref, d_ref), third)
    gamma, delta = a_ref[HALF : HALF + 1, :wide], a_ref[HALF : HALF + 1, wide:]
    alpha = gamma / delta
    precond = precond_ref[...] - alpha * second_ref[...]
    gamma_next = summed((right_ref[...] - alpha * image_ref[...]) * precond)
    delta_next = summed((image_ref[...] - alpha * third[...]) * precond)
    line = jnp.concatenate([gamma_next, delta_next], axis=1)
    dots_ref[...] = jnp.broadcast_to(line, dots_ref.shape)


def last_kernel(spot_ref, e_ref, f_ref, g_ref, h_ref, a_ref, b_ref, c_ref, d_ref, right_ref, precond_ref, image_ref, second_ref, solution_ref, residual_ref, third):
    wide = right_ref.shape[1]
    take_rows(spot_ref[0], (a_ref, b_ref, c_ref, d_ref), third)
    gamma, delta = a_ref[HALF : HALF + 1, :wide], a_ref[HALF : HALF + 1, wide:]
    alpha = gamma / delta
    dots = (e_ref[...] + f_ref[...] + g_ref[...] + h_ref[...])[0:1]
    gamma_next, delta_next = dots[:, :wide], dots[:, wide:]
    beta = gamma_next / gamma
    step = gamma_next / (delta_next - beta * gamma_next / alpha)
    for t in range(right_ref.shape[0] // TILE):
        rows = pl.ds(t * TILE, TILE)
        u, w = precond_ref[rows, :], image_ref[rows, :]
        u_next = u - alpha * second_ref[rows, :]
        w_next = w - alpha * third[rows, :]
        solution_ref[:, rows] = (alpha * u + step * (u_next + beta * u)).T
        residual_ref[:, rows] = ((right_ref[rows, :] - alpha * w) - step * (w_next + beta * w)).T


def shaped(*dims):
    return jax.ShapeDtypeStruct(dims, jnp.float32)


def close(*dims):
    return pltpu.VMEM(dims, jnp.float32)


def near(*arrays):
    return [pltpu.with_memory_space_constraint(a, pltpu.VMEM) for a in arrays]


SMEM = pl.BlockSpec(memory_space=pltpu.SMEM)
VMEM = pl.BlockSpec(memory_space=pltpu.VMEM)
ANY = pl.BlockSpec(memory_space=pl.ANY)


def added_over_col(array):
    both = array + other_core(array)
    around = [step_y(both, step) for step in STEPS]
    return both + around[0] + around[1] + around[2]


def spread_out(packed):
    own = into_column(added_over_col(packed))
    return near(own, *[step_x(own, step) for step in STEPS])


def body(normal_matrix, right_side, tile_inverse, order_ids):
    block_rows, block_cols = normal_matrix.shape
    wide = right_side.shape[1]
    count = tile_inverse.shape[0]
    spot = jnp.stack([lax.axis_index("row") % X, lax.axis_index("col")]).astype(jnp.int32)
    vector = shaped(block_cols, wide)
    square = close(count, TILE, TILE)
    tall = close(block_cols, wide)
    block = close(block_rows, block_cols)
    packed_shape = close(HALF + LINES, 2 * wide)

    packed, right, precond, masked = pl.pallas_call(
        first_kernel,
        out_shape=(packed_shape, vector, vector, shaped(count, TILE, TILE)),
        in_specs=[VMEM, ANY, ANY, ANY],
        out_specs=(VMEM, ANY, ANY, ANY),
        scratch_shapes=[close(wide, block_cols), square, block, tall, tall, square, pltpu.SemaphoreType.DMA((5,)), pltpu.SemaphoreType.DMA((3,))],
    )(order_ids.reshape(count, TILE), right_side.T, tile_inverse, normal_matrix)
    blocks = spread_out(packed)

    packed, image, second = pl.pallas_call(
        second_kernel,
        out_shape=(packed_shape, vector, vector),
        in_specs=[SMEM] + [VMEM] * 4 + [ANY] * 3,
        out_specs=(VMEM, ANY, ANY),
        scratch_shapes=[tall, square, block, tall, tall, pltpu.SemaphoreType.DMA((5,)), pltpu.SemaphoreType.DMA((2,))],
    )(spot, *blocks, precond, masked, normal_matrix)
    blocks = spread_out(packed)
    vectors = near(right, precond, image, second)

    dots = pl.pallas_call(
        third_kernel,
        out_shape=close(LINES, 2 * wide),
        in_specs=[SMEM] + [VMEM] * 8,
        scratch_shapes=[tall],
    )(spot, *blocks, *vectors)

    dots = dots + other_core(dots)
    flat = shaped(wide, block_cols)
    solution, residual = pl.pallas_call(
        last_kernel,
        out_shape=(flat, flat),
        in_specs=[SMEM] + [VMEM] * 12,
        scratch_shapes=[tall],
    )(spot, *near(dots, *[step_y(dots, step) for step in STEPS]), *blocks, *vectors)
    return solution.T, residual.T


def solution(mesh):
    return jax.shard_map(
        body,
        mesh=mesh,
        in_specs=(P("row", "col"), P("col", None), P("col", None, None), P("col")),
        out_specs=(P("col", None), P("col", None)),
        check_vma=False,
    )
```

```python
import jax
import jax.numpy as jnp
from jax import lax
from jax.experimental import pallas as pl
from jax.experimental.pallas import tpu as pltpu
from jax.sharding import PartitionSpec as P


BOTH = ("row", "col")
Z, X, Y, K = 8, 4, 4, 2
COLS = Y * K
TILE = 128
HALF = 144
LINES = 8
REACH = (3, 1, 0, 2)
STEPS = (1, 3, 2)


def place(z, x, y, k):
    return ((z % Z) * X + x % X) * COLS + (y % Y) * K + k % K


def everyone():
    return [(z, x, y, k) for z in range(Z) for x in range(X) for y in range(Y) for k in range(K)]


def moved(array, to):
    pairs = [(place(*at), place(*to(*at))) for at in everyone()]
    return lax.ppermute(array, BOTH, pairs)


def other_core(array):
    return moved(array, lambda z, x, y, k: (z, x, y, k + 1))


def step_y(array, step):
    return moved(array, lambda z, x, y, k: (z, x, y + step, k))


def step_x(array, step):
    return moved(array, lambda z, x, y, k: (z, x + step, y, k))


def hop(plane, y, k):
    reach = REACH[(y - plane // K) % Y]
    return 1 + reach if k else -reach


def into_column(array):
    return moved(array, lambda z, x, y, k: (z + hop(z, y, k), x, z // K, z % K))


def parts_of(a):
    top = a.astype(jnp.bfloat16)
    rest = a - top.astype(jnp.float32)
    mid = rest.astype(jnp.bfloat16)
    return top, mid, (rest - mid.astype(jnp.float32)).astype(jnp.bfloat16)


def pass_of(a, b):
    return jnp.dot(a, b, preferred_element_type=jnp.float32)


def product(left, right):
    n = right.shape[1]
    top, mid, low = parts_of(left)
    side = jnp.concatenate(parts_of(right), axis=1)
    one = pass_of(top, side)
    two = pass_of(mid, side[:, : 2 * n])
    three = pass_of(low, side[:, :n])
    return one[:, :n] + ((one[:, n : 2 * n] + two[:, :n]) + ((one[:, 2 * n :] + two[:, n:]) + three))


def dot(a, b):
    return jnp.dot(a, b, precision=lax.Precision.HIGHEST, preferred_element_type=jnp.float32)


def summed(a):
    return jnp.sum(a, axis=0, keepdims=True)


def put_rows(value, line, packed_ref):
    packed_ref[0:HALF, :] = jnp.concatenate([value[:HALF], value[HALF:]], axis=1)
    packed_ref[HALF:, :] = jnp.broadcast_to(line, (LINES, line.shape[1]))


def take_rows(x, block_refs, out_ref):
    wide = out_ref.shape[1]
    for step, ref in zip((0,) + STEPS, block_refs):
        at = pl.multiple_of(lax.rem(x + X - step, X) * (2 * HALF), 8)
        block = ref[0:HALF, :]
        out_ref[pl.ds(at, HALF), :] = block[:, :wide]
        out_ref[pl.ds(at + HALF, HALF), :] = block[:, wide:]


def copies_of(sources, targets, sems):
    return [pltpu.make_async_copy(s, t, sems.at[i]) for i, (s, t) in enumerate(zip(sources, targets))]


def thirds(ref):
    return [ref.at[pl.ds(3 * i, 3)] for i in range(ref.shape[0] // 3)]


def first_kernel(order_hbm, flat_hbm, tile_hbm, matrix_hbm, packed_ref, right, precond, masked, matrix, order_ref, flat, tiles, in_sems):
    arrivals = copies_of([order_hbm, flat_hbm, *thirds(tile_hbm), matrix_hbm], [order_ref, flat, *thirds(tiles), matrix], in_sems)
    for copy in arrivals:
        copy.start()
    eye = lax.broadcasted_iota(jnp.int32, (TILE, TILE), 0) == lax.broadcasted_iota(jnp.int32, (TILE, TILE), 1)
    wide = flat.shape[0]
    spans = [slice(t * TILE, (t + 1) * TILE) for t in range(tiles.shape[0])]
    arrivals[0].wait()
    across = [jnp.broadcast_to(order_ref[t : t + 1, :].astype(jnp.float32), (TILE, TILE)) for t in range(len(spans))]
    diagonal = jnp.concatenate([jnp.where(eye, a, 0.0).astype(jnp.bfloat16) for a in across], axis=0)
    down = pass_of(diagonal, jnp.ones((TILE, TILE), jnp.bfloat16))
    for copy in arrivals[1:-1]:
        copy.wait()
    sides = [flat[:, span].T for span in spans]
    kept = [jnp.where(across[t] == down[span], tiles[t], 0.0) for t, span in enumerate(spans)]
    owns = [dot(tile, side) for tile, side in zip(kept, sides)]
    gamma = jnp.zeros((8, wide), jnp.float32)
    for side, own in zip(sides, owns):
        gamma = gamma + jnp.sum((side * own).reshape(TILE // 8, 8, wide), axis=0)
    gamma = summed(gamma)
    for t, span in enumerate(spans):
        masked[t] = kept[t]
        right[span, :] = sides[t]
        precond[span, :] = owns[t]
    arrivals[-1].wait()
    put_rows(product(matrix[...], precond[...]), jnp.concatenate([gamma, jnp.zeros_like(gamma)], axis=1), packed_ref)


def second_kernel(spot_ref, a_ref, b_ref, c_ref, d_ref, precond_ref, masked_ref, matrix_ref, packed_ref, image, second):
    wide = image.shape[1]
    take_rows(spot_ref[0] // COLS % X, (a_ref, b_ref, c_ref, d_ref), image)
    spans = [slice(t * TILE, (t + 1) * TILE) for t in range(masked_ref.shape[0])]
    images = [image[span, :] for span in spans]
    seconds = [dot(masked_ref[t], images[t]) for t in range(len(spans))]
    for span, value in zip(spans, seconds):
        second[span, :] = value
    delta = summed(image[...] * precond_ref[...])
    gamma = jnp.where(spot_ref[0] % COLS == 0, a_ref[HALF : HALF + 1, :wide], 0.0)
    put_rows(product(matrix_ref[...], second[...]), jnp.concatenate([gamma, delta], axis=1), packed_ref)


def third_kernel(spot_ref, a_ref, b_ref, c_ref, d_ref, right_ref, precond_ref, image_ref, second_ref, dots_ref, third):
    wide = right_ref.shape[1]
    take_rows(spot_ref[0] // COLS % X, (a_ref, b_ref, c_ref, d_ref), third)
    gamma, delta = a_ref[HALF : HALF + 1, :wide], a_ref[HALF : HALF + 1, wide:]
    alpha = gamma / delta
    precond = precond_ref[...] - alpha * second_ref[...]
    gamma_next = summed((right_ref[...] - alpha * image_ref[...]) * precond)
    delta_next = summed((image_ref[...] - alpha * third[...]) * precond)
    line = jnp.concatenate([gamma_next, delta_next], axis=1)
    dots_ref[...] = jnp.broadcast_to(line, dots_ref.shape)


def last_kernel(spot_ref, e_ref, f_ref, g_ref, h_ref, a_ref, b_ref, c_ref, d_ref, right_ref, precond_ref, image_ref, second_ref, solution_ref, residual_ref, third):
    wide = right_ref.shape[1]
    take_rows(spot_ref[0] // COLS % X, (a_ref, b_ref, c_ref, d_ref), third)
    gamma, delta = a_ref[HALF : HALF + 1, :wide], a_ref[HALF : HALF + 1, wide:]
    alpha = gamma / delta
    dots = (e_ref[...] + f_ref[...] + g_ref[...] + h_ref[...])[0:1]
    gamma_next, delta_next = dots[:, :wide], dots[:, wide:]
    beta = gamma_next / gamma
    step = gamma_next / (delta_next - beta * gamma_next / alpha)
    for t in range(right_ref.shape[0] // TILE):
        rows = pl.ds(t * TILE, TILE)
        u, w = precond_ref[rows, :], image_ref[rows, :]
        u_next = u - alpha * second_ref[rows, :]
        w_next = w - alpha * third[rows, :]
        solution_ref[:, rows] = (alpha * u + step * (u_next + beta * u)).T
        residual_ref[:, rows] = ((right_ref[rows, :] - alpha * w) - step * (w_next + beta * w)).T


def shaped(*dims):
    return jax.ShapeDtypeStruct(dims, jnp.float32)


def close(*dims):
    return pltpu.VMEM(dims, jnp.float32)


def near(*arrays):
    return [pltpu.with_memory_space_constraint(a, pltpu.VMEM) for a in arrays]


def far(*arrays):
    return [pltpu.with_memory_space_constraint(a, pltpu.HBM) for a in arrays]


PARAMS = pltpu.CompilerParams(vmem_limit_bytes=12 << 20)
SMEM = pl.BlockSpec(memory_space=pltpu.SMEM)
VMEM = pl.BlockSpec(memory_space=pltpu.VMEM)
HBM = pl.BlockSpec(memory_space=pltpu.HBM)


def added_over_col(array):
    both = array + other_core(array)
    around = [step_y(both, step) for step in STEPS]
    return both + around[0] + around[1] + around[2]


def spread_out(packed, *arrays):
    own = into_column(added_over_col(packed))
    return near(own, *[step_x(own, step) for step in STEPS]), near(*arrays)


def body(normal_matrix, right_side, tile_inverse, order_ids):
    block_rows, block_cols = normal_matrix.shape
    wide = right_side.shape[1]
    count = tile_inverse.shape[0]
    spot = lax.axis_index(BOTH).astype(jnp.int32).reshape(1)
    square = close(count, TILE, TILE)
    tall = close(block_cols, wide)
    packed_shape = close(HALF + LINES, 2 * wide)

    packed, right, precond, masked, matrix = pl.pallas_call(
        first_kernel,
        compiler_params=PARAMS,
        out_shape=(packed_shape, tall, tall, square, close(block_rows, block_cols)),
        in_specs=[HBM] * 4,
        scratch_shapes=[pltpu.VMEM((count, TILE), jnp.int32), close(wide, block_cols), square, pltpu.SemaphoreType.DMA((6,))],
    )(*far(order_ids.reshape(count, TILE), right_side.T, tile_inverse, normal_matrix))
    blocks, (precond, masked, matrix) = spread_out(packed, precond, masked, matrix)

    packed, image, second = pl.pallas_call(
        second_kernel,
        compiler_params=PARAMS,
        out_shape=(packed_shape, tall, tall),
        in_specs=[SMEM] + [VMEM] * 7,
    )(spot, *blocks, precond, masked, matrix)
    blocks, vectors = spread_out(packed, right, precond, image, second)

    dots = pl.pallas_call(
        third_kernel,
        compiler_params=PARAMS,
        out_shape=close(LINES, 2 * wide),
        in_specs=[SMEM] + [VMEM] * 8,
        scratch_shapes=[tall],
    )(spot, *blocks, *vectors)

    dots = dots + other_core(dots)
    flat = shaped(wide, block_cols)
    solution, residual = pl.pallas_call(
        last_kernel,
        compiler_params=PARAMS,
        out_shape=(flat, flat),
        in_specs=[SMEM] + [VMEM] * 12,
        scratch_shapes=[tall],
    )(spot, *near(dots, *[step_y(dots, step) for step in STEPS]), *blocks, *vectors)
    return solution.T, residual.T


def solution(mesh):
    return jax.shard_map(
        body,
        mesh=mesh,
        in_specs=(P("row", "col"), P("col", None), P("col", None, None), P("col")),
        out_specs=(P("col", None), P("col", None)),
        check_vma=False,
    )
```

```python
import jax
import jax.numpy as jnp
from jax import lax
from jax.experimental import pallas as pl
from jax.experimental.pallas import tpu as pltpu
from jax.sharding import Mesh, PartitionSpec as P


AXES = ("z", "x", "y", "k")
Z, X, Y, K = 8, 4, 4, 2
COLS = Y * K
TILE = 128
HALF = 144
LINES = 8
REACH = (3, 1, 0, 2)
STEPS = (1, 3, 2)


def place(z, x, y, k):
    return ((z % Z) * X + x % X) * COLS + (y % Y) * K + k % K


def everyone():
    return [(z, x, y, k) for z in range(Z) for x in range(X) for y in range(Y) for k in range(K)]


def moved(array, to):
    pairs = [(place(*at), place(*to(*at))) for at in everyone()]
    return lax.ppermute(array, AXES, pairs)


def other_core(array):
    return moved(array, lambda z, x, y, k: (z, x, y, k + 1))


def step_y(array, step):
    return moved(array, lambda z, x, y, k: (z, x, y + step, k))


def step_x(array, step):
    return moved(array, lambda z, x, y, k: (z, x + step, y, k))


def hop(plane, y, k):
    reach = REACH[(y - plane // K) % Y]
    return 1 + reach if k else -reach


def into_column(array):
    return moved(array, lambda z, x, y, k: (z + hop(z, y, k), x, z // K, z % K))


def parts_of(a):
    top = a.astype(jnp.bfloat16)
    rest = a - top.astype(jnp.float32)
    mid = rest.astype(jnp.bfloat16)
    return top, mid, (rest - mid.astype(jnp.float32)).astype(jnp.bfloat16)


def pass_of(a, b):
    return jnp.dot(a, b, preferred_element_type=jnp.float32)


def product(left, right):
    n = right.shape[1]
    top, mid, low = parts_of(left)
    side = jnp.concatenate(parts_of(right), axis=1)
    one = pass_of(top, side)
    two = pass_of(mid, side[:, : 2 * n])
    three = pass_of(low, side[:, :n])
    return one[:, :n] + ((one[:, n : 2 * n] + two[:, :n]) + ((one[:, 2 * n :] + two[:, n:]) + three))


def dot(a, b):
    return jnp.dot(a, b, precision=lax.Precision.HIGHEST, preferred_element_type=jnp.float32)


def summed(a):
    return jnp.sum(a, axis=0, keepdims=True)


def put_rows(value, line, packed_ref):
    packed_ref[0:HALF, :] = jnp.concatenate([value[:HALF], value[HALF:]], axis=1)
    packed_ref[HALF:, :] = jnp.broadcast_to(line, (LINES, line.shape[1]))


def take_rows(x, block_refs, out_ref):
    wide = out_ref.shape[1]
    for step, ref in zip((0,) + STEPS, block_refs):
        at = pl.multiple_of(lax.rem(x + X - step, X) * (2 * HALF), 8)
        block = ref[0:HALF, :]
        out_ref[pl.ds(at, HALF), :] = block[:, :wide]
        out_ref[pl.ds(at + HALF, HALF), :] = block[:, wide:]


def copies_of(sources, targets, sems):
    return [pltpu.make_async_copy(s, t, sems.at[i]) for i, (s, t) in enumerate(zip(sources, targets))]


def thirds(ref):
    return [ref.at[pl.ds(3 * i, 3)] for i in range(ref.shape[0] // 3)]


def first_kernel(order_hbm, flat_hbm, tile_hbm, matrix_hbm, packed_ref, right, precond, masked, matrix, order_ref, flat, tiles, in_sems):
    arrivals = copies_of([order_hbm, flat_hbm, *thirds(tile_hbm), matrix_hbm], [order_ref, flat, *thirds(tiles), matrix], in_sems)
    for copy in arrivals:
        copy.start()
    eye = lax.broadcasted_iota(jnp.int32, (TILE, TILE), 0) == lax.broadcasted_iota(jnp.int32, (TILE, TILE), 1)
    wide = flat.shape[0]
    spans = [slice(t * TILE, (t + 1) * TILE) for t in range(tiles.shape[0])]
    arrivals[0].wait()
    across = [jnp.broadcast_to(order_ref[t : t + 1, :].astype(jnp.float32), (TILE, TILE)) for t in range(len(spans))]
    diagonal = jnp.concatenate([jnp.where(eye, a, 0.0).astype(jnp.bfloat16) for a in across], axis=0)
    down = pass_of(diagonal, jnp.ones((TILE, TILE), jnp.bfloat16))
    for copy in arrivals[1:-1]:
        copy.wait()
    sides = [flat[:, span].T for span in spans]
    kept = [jnp.where(across[t] == down[span], tiles[t], 0.0) for t, span in enumerate(spans)]
    owns = [dot(tile, side) for tile, side in zip(kept, sides)]
    gamma = jnp.zeros((8, wide), jnp.float32)
    for side, own in zip(sides, owns):
        gamma = gamma + jnp.sum((side * own).reshape(TILE // 8, 8, wide), axis=0)
    gamma = summed(gamma)
    for t, span in enumerate(spans):
        masked[t] = kept[t]
        right[span, :] = sides[t]
        precond[span, :] = owns[t]
    arrivals[-1].wait()
    put_rows(product(matrix[...], precond[...]), jnp.concatenate([gamma, jnp.zeros_like(gamma)], axis=1), packed_ref)


def second_kernel(spot_ref, a_ref, b_ref, c_ref, d_ref, precond_ref, masked_ref, matrix_ref, packed_ref, image, second):
    wide = image.shape[1]
    take_rows(spot_ref[0] // COLS % X, (a_ref, b_ref, c_ref, d_ref), image)
    spans = [slice(t * TILE, (t + 1) * TILE) for t in range(masked_ref.shape[0])]
    images = [image[span, :] for span in spans]
    seconds = [dot(masked_ref[t], images[t]) for t in range(len(spans))]
    for span, value in zip(spans, seconds):
        second[span, :] = value
    delta = summed(image[...] * precond_ref[...])
    gamma = jnp.where(spot_ref[0] % COLS == 0, a_ref[HALF : HALF + 1, :wide], 0.0)
    put_rows(product(matrix_ref[...], second[...]), jnp.concatenate([gamma, delta], axis=1), packed_ref)


def third_kernel(spot_ref, own_ref, right_ref, precond_ref, image_ref, second_ref, dots_ref):
    wide = right_ref.shape[1]
    gamma, delta = own_ref[HALF : HALF + 1, :wide], own_ref[HALF : HALF + 1, wide:]
    alpha = gamma / delta
    first = spot_ref[0] // COLS % X * (2 * HALF)
    total = [jnp.zeros((1, wide), jnp.float32)] * 2
    for part in range(2):
        rows = pl.ds(pl.multiple_of(first + part * HALF, 8), HALF)
        third = own_ref[0:HALF, part * wide : (part + 1) * wide]
        precond = precond_ref[rows, :] - alpha * second_ref[rows, :]
        residual = right_ref[rows, :] - alpha * image_ref[rows, :]
        image = image_ref[rows, :] - alpha * third
        total = [total[0] + summed(residual * precond), total[1] + summed(image * precond)]
    dots_ref[...] = jnp.concatenate(total, axis=1)


def last_kernel(spot_ref, dots_ref, a_ref, b_ref, c_ref, d_ref, right_ref, precond_ref, image_ref, second_ref, solution_ref, residual_ref, third):
    wide = right_ref.shape[1]
    take_rows(spot_ref[0] // COLS % X, (a_ref, b_ref, c_ref, d_ref), third)
    gamma, delta = a_ref[HALF : HALF + 1, :wide], a_ref[HALF : HALF + 1, wide:]
    alpha = gamma / delta
    dots = jnp.sum(dots_ref[...], axis=0)
    gamma_next, delta_next = dots[:, :wide], dots[:, wide:]
    beta = gamma_next / gamma
    step = gamma_next / (delta_next - beta * gamma_next / alpha)
    for t in range(right_ref.shape[0] // TILE):
        rows = pl.ds(t * TILE, TILE)
        u, w = precond_ref[rows, :], image_ref[rows, :]
        u_next = u - alpha * second_ref[rows, :]
        w_next = w - alpha * third[rows, :]
        solution_ref[:, rows] = (alpha * u + step * (u_next + beta * u)).T
        residual_ref[:, rows] = ((right_ref[rows, :] - alpha * w) - step * (w_next + beta * w)).T


def shaped(*dims):
    return jax.ShapeDtypeStruct(dims, jnp.float32)


def close(*dims):
    return pltpu.VMEM(dims, jnp.float32)


def near(*arrays):
    return [pltpu.with_memory_space_constraint(a, pltpu.VMEM) for a in arrays]


def far(*arrays):
    return [pltpu.with_memory_space_constraint(a, pltpu.HBM) for a in arrays]


PARAMS = pltpu.CompilerParams(vmem_limit_bytes=12 << 20)
SMEM = pl.BlockSpec(memory_space=pltpu.SMEM)
VMEM = pl.BlockSpec(memory_space=pltpu.VMEM)
HBM = pl.BlockSpec(memory_space=pltpu.HBM)


def added_over_col(array):
    both = array + other_core(array)
    around = [step_y(both, step) for step in STEPS]
    return both + around[0] + around[1] + around[2]


def spread_out(packed, *arrays):
    own = into_column(added_over_col(packed))
    return near(own, *[step_x(own, step) for step in STEPS]), near(*arrays)


def body(normal_matrix, right_side, tile_inverse, order_ids):
    block_rows, block_cols = normal_matrix.shape
    wide = right_side.shape[1]
    count = tile_inverse.shape[0]
    spot = lax.axis_index(AXES).astype(jnp.int32).reshape(1)
    square = close(count, TILE, TILE)
    tall = close(block_cols, wide)
    packed_shape = close(HALF + LINES, 2 * wide)

    packed, right, precond, masked, matrix = pl.pallas_call(
        first_kernel,
        compiler_params=PARAMS,
        out_shape=(packed_shape, tall, tall, square, close(block_rows, block_cols)),
        in_specs=[HBM] * 4,
        scratch_shapes=[pltpu.VMEM((count, TILE), jnp.int32), close(wide, block_cols), square, pltpu.SemaphoreType.DMA((6,))],
    )(*far(order_ids.reshape(count, TILE), right_side.T, tile_inverse, normal_matrix))
    blocks, (precond, masked, matrix) = spread_out(packed, precond, masked, matrix)

    packed, image, second = pl.pallas_call(
        second_kernel,
        compiler_params=PARAMS,
        out_shape=(packed_shape, tall, tall),
        in_specs=[SMEM] + [VMEM] * 7,
    )(spot, *blocks, precond, masked, matrix)
    blocks, vectors = spread_out(packed, right, precond, image, second)

    dots = pl.pallas_call(
        third_kernel,
        compiler_params=PARAMS,
        out_shape=close(1, 2 * wide),
        in_specs=[SMEM] + [VMEM] * 5,
    )(spot, blocks[0], *vectors)

    plane = jnp.broadcast_to(dots, (X * COLS, *dots.shape))
    plane = lax.all_to_all(plane, ("x", "y", "k"), 0, 0, tiled=True)
    flat = shaped(wide, block_cols)
    solution, residual = pl.pallas_call(
        last_kernel,
        compiler_params=PARAMS,
        out_shape=(flat, flat),
        in_specs=[SMEM] + [VMEM] * 9,
        scratch_shapes=[tall],
    )(spot, *near(plane), *blocks, *vectors)
    return solution.T, residual.T


def solution(mesh):
    rows, cols = AXES[:2], AXES[2:]
    return jax.shard_map(
        body,
        mesh=Mesh(mesh.devices.reshape(Z, X, Y, K), AXES),
        in_specs=(P(rows, cols), P(cols, None), P(cols, None, None), P(cols)),
        out_specs=(P(cols, None), P(cols, None)),
        check_vma=False,
    )
```

```python
import jax
import jax.numpy as jnp
from jax import lax
from jax.experimental import pallas as pl
from jax.experimental.pallas import tpu as pltpu
from jax.sharding import Mesh, PartitionSpec as P


AXES = ("z", "x", "y", "k")
Z, X, Y, K = 8, 4, 4, 2
COLS = Y * K
TILE = 128
HALF = 144
LINES = 8
REACH = (3, 1, 0, 2)
STEPS = (1, 3, 2)


def place(z, x, y, k):
    return ((z % Z) * X + x % X) * COLS + (y % Y) * K + k % K


def everyone():
    return [(z, x, y, k) for z in range(Z) for x in range(X) for y in range(Y) for k in range(K)]


def moved(array, to):
    pairs = [(place(*at), place(*to(*at))) for at in everyone()]
    return lax.ppermute(array, AXES, pairs)


def other_core(array):
    return moved(array, lambda z, x, y, k: (z, x, y, k + 1))


def step_y(array, step):
    return moved(array, lambda z, x, y, k: (z, x, y + step, k))


def step_x(array, step):
    return moved(array, lambda z, x, y, k: (z, x + step, y, k))


def hop(plane, y, k):
    reach = REACH[(y - plane // K) % Y]
    return 1 + reach if k else -reach


def into_column(array):
    return moved(array, lambda z, x, y, k: (z + hop(z, y, k), x, z // K, z % K))


def parts_of(a):
    top = a.astype(jnp.bfloat16)
    rest = a - top.astype(jnp.float32)
    mid = rest.astype(jnp.bfloat16)
    return top, mid, (rest - mid.astype(jnp.float32)).astype(jnp.bfloat16)


def pass_of(a, b):
    return jnp.dot(a, b, preferred_element_type=jnp.float32)


def product(left, right):
    n = right.shape[1]
    top, mid, low = parts_of(left)
    side = jnp.concatenate(parts_of(right), axis=1)
    one = pass_of(top, side)
    two = pass_of(mid, side[:, : 2 * n])
    three = pass_of(low, side[:, :n])
    return one[:, :n] + ((one[:, n : 2 * n] + two[:, :n]) + ((one[:, 2 * n :] + two[:, n:]) + three))


def dot(a, b):
    return jnp.dot(a, b, precision=lax.Precision.HIGHEST, preferred_element_type=jnp.float32)


def summed(a):
    return jnp.sum(a, axis=0, keepdims=True)


def put_rows(value, line, packed_ref):
    packed_ref[0:HALF, :] = jnp.concatenate([value[:HALF], value[HALF:]], axis=1)
    packed_ref[HALF:, :] = jnp.broadcast_to(line, (LINES, line.shape[1]))


def take_rows(x, block_refs, out_ref):
    wide = out_ref.shape[1]
    for step, ref in zip((0,) + STEPS, block_refs):
        at = pl.multiple_of(lax.rem(x + X - step, X) * (2 * HALF), 8)
        block = ref[0:HALF, :]
        out_ref[pl.ds(at, HALF), :] = block[:, :wide]
        out_ref[pl.ds(at + HALF, HALF), :] = block[:, wide:]


def copies_of(sources, targets, sems):
    return [pltpu.make_async_copy(s, t, sems.at[i]) for i, (s, t) in enumerate(zip(sources, targets))]


def thirds(ref):
    return [ref.at[pl.ds(3 * i, 3)] for i in range(ref.shape[0] // 3)]


def first_kernel(order_hbm, flat_hbm, tile_hbm, matrix_hbm, packed_ref, right, precond, masked, matrix, order_ref, flat, tiles, in_sems):
    arrivals = copies_of([order_hbm, flat_hbm, *thirds(tile_hbm), matrix_hbm], [order_ref, flat, *thirds(tiles), matrix], in_sems)
    for copy in arrivals:
        copy.start()
    eye = lax.broadcasted_iota(jnp.int32, (TILE, TILE), 0) == lax.broadcasted_iota(jnp.int32, (TILE, TILE), 1)
    wide = flat.shape[0]
    spans = [slice(t * TILE, (t + 1) * TILE) for t in range(tiles.shape[0])]
    arrivals[0].wait()
    across = [jnp.broadcast_to(order_ref[t : t + 1, :].astype(jnp.float32), (TILE, TILE)) for t in range(len(spans))]
    diagonal = jnp.concatenate([jnp.where(eye, a, 0.0).astype(jnp.bfloat16) for a in across], axis=0)
    down = pass_of(diagonal, jnp.ones((TILE, TILE), jnp.bfloat16))
    for copy in arrivals[1:-1]:
        copy.wait()
    sides = [flat[:, span].T for span in spans]
    kept = [jnp.where(across[t] == down[span], tiles[t], 0.0) for t, span in enumerate(spans)]
    owns = [dot(tile, side) for tile, side in zip(kept, sides)]
    gamma = jnp.zeros((8, wide), jnp.float32)
    for side, own in zip(sides, owns):
        gamma = gamma + jnp.sum((side * own).reshape(TILE // 8, 8, wide), axis=0)
    gamma = summed(gamma)
    for t, span in enumerate(spans):
        masked[t] = kept[t]
        right[span, :] = sides[t]
        precond[span, :] = owns[t]
    arrivals[-1].wait()
    put_rows(product(matrix[...], precond[...]), jnp.concatenate([gamma, jnp.zeros_like(gamma)], axis=1), packed_ref)


def second_kernel(spot_ref, a_ref, b_ref, c_ref, d_ref, precond_ref, masked_ref, matrix_ref, packed_ref, image, second):
    wide = image.shape[1]
    take_rows(spot_ref[0] // COLS % X, (a_ref, b_ref, c_ref, d_ref), image)
    spans = [slice(t * TILE, (t + 1) * TILE) for t in range(masked_ref.shape[0])]
    images = [image[span, :] for span in spans]
    seconds = [dot(masked_ref[t], images[t]) for t in range(len(spans))]
    for span, value in zip(spans, seconds):
        second[span, :] = value
    delta = summed(image[...] * precond_ref[...])
    gamma = jnp.where(spot_ref[0] % COLS == 0, a_ref[HALF : HALF + 1, :wide], 0.0)
    put_rows(product(matrix_ref[...], second[...]), jnp.concatenate([gamma, delta], axis=1), packed_ref)


def third_kernel(spot_ref, own_ref, right_ref, precond_ref, image_ref, second_ref, dots_ref):
    wide = right_ref.shape[1]
    gamma, delta = own_ref[HALF : HALF + 1, :wide], own_ref[HALF : HALF + 1, wide:]
    alpha = gamma / delta
    first = spot_ref[0] // COLS % X * (2 * HALF)
    total = [jnp.zeros((1, wide), jnp.float32)] * 2
    for part in range(2):
        rows = pl.ds(pl.multiple_of(first + part * HALF, 8), HALF)
        third = own_ref[0:HALF, part * wide : (part + 1) * wide]
        precond = precond_ref[rows, :] - alpha * second_ref[rows, :]
        residual = right_ref[rows, :] - alpha * image_ref[rows, :]
        image = image_ref[rows, :] - alpha * third
        total = [total[0] + summed(residual * precond), total[1] + summed(image * precond)]
    dots_ref[...] = jnp.concatenate(total, axis=1)


def last_kernel(spot_ref, dots_ref, a_ref, b_ref, c_ref, d_ref, right_ref, precond_ref, image_ref, second_ref, solution_hbm, residual_hbm, third, solution, residual, sems):
    wide = right_ref.shape[1]
    take_rows(spot_ref[0] // COLS % X, (a_ref, b_ref, c_ref, d_ref), third)
    gamma, delta = a_ref[HALF : HALF + 1, :wide], a_ref[HALF : HALF + 1, wide:]
    alpha = gamma / delta
    dots = jnp.sum(dots_ref[...], axis=0)
    gamma_next, delta_next = dots[:, :wide], dots[:, wide:]
    beta = gamma_next / gamma
    step = gamma_next / (delta_next - beta * gamma_next / alpha)
    kappa = alpha + (step + step * beta)
    cross = step * alpha
    count = right_ref.shape[0] // TILE
    leaving = []
    for t in range(count):
        rows = pl.ds(t * TILE, TILE)
        solution[:, rows] = (kappa * precond_ref[rows, :] - cross * second_ref[rows, :]).T
        residual[:, rows] = ((right_ref[rows, :] - kappa * image_ref[rows, :]) + cross * third[rows, :]).T
        if t % 3 == 2:
            done = pl.ds((t - 2) * TILE, 3 * TILE)
            for source, target in ((solution, solution_hbm), (residual, residual_hbm)):
                leaving.append(pltpu.make_async_copy(source.at[:, done], target.at[:, done], sems.at[len(leaving)]))
                leaving[-1].start()
    for copy in leaving:
        copy.wait()


def shaped(*dims):
    return jax.ShapeDtypeStruct(dims, jnp.float32)


def close(*dims):
    return pltpu.VMEM(dims, jnp.float32)


def near(*arrays):
    return [pltpu.with_memory_space_constraint(a, pltpu.VMEM) for a in arrays]


def far(*arrays):
    return [pltpu.with_memory_space_constraint(a, pltpu.HBM) for a in arrays]


PARAMS = pltpu.CompilerParams(vmem_limit_bytes=12 << 20)
SMEM = pl.BlockSpec(memory_space=pltpu.SMEM)
VMEM = pl.BlockSpec(memory_space=pltpu.VMEM)
HBM = pl.BlockSpec(memory_space=pltpu.HBM)


def added_over_col(array):
    both = array + other_core(array)
    around = [step_y(both, step) for step in STEPS]
    return both + around[0] + around[1] + around[2]


def spread_out(packed, *arrays):
    own = into_column(added_over_col(packed))
    return near(own, *[step_x(own, step) for step in STEPS]), near(*arrays)


def body(normal_matrix, right_side, tile_inverse, order_ids):
    block_rows, block_cols = normal_matrix.shape
    wide = right_side.shape[1]
    count = tile_inverse.shape[0]
    spot = lax.axis_index(AXES).astype(jnp.int32).reshape(1)
    square = close(count, TILE, TILE)
    tall = close(block_cols, wide)
    packed_shape = close(HALF + LINES, 2 * wide)

    packed, right, precond, masked, matrix = pl.pallas_call(
        first_kernel,
        compiler_params=PARAMS,
        out_shape=(packed_shape, tall, tall, square, close(block_rows, block_cols)),
        in_specs=[HBM] * 4,
        scratch_shapes=[pltpu.VMEM((count, TILE), jnp.int32), close(wide, block_cols), square, pltpu.SemaphoreType.DMA((6,))],
    )(*far(order_ids.reshape(count, TILE), right_side.T, tile_inverse, normal_matrix))
    blocks, (precond, masked, matrix) = spread_out(packed, precond, masked, matrix)

    packed, image, second = pl.pallas_call(
        second_kernel,
        compiler_params=PARAMS,
        out_shape=(packed_shape, tall, tall),
        in_specs=[SMEM] + [VMEM] * 7,
    )(spot, *blocks, precond, masked, matrix)
    blocks, vectors = spread_out(packed, right, precond, image, second)

    dots = pl.pallas_call(
        third_kernel,
        compiler_params=PARAMS,
        out_shape=close(1, 2 * wide),
        in_specs=[SMEM] + [VMEM] * 5,
    )(spot, blocks[0], *vectors)

    plane = jnp.broadcast_to(dots, (X * COLS, *dots.shape))
    plane = lax.all_to_all(plane, ("x", "y", "k"), 0, 0, tiled=True)
    flat = shaped(wide, block_cols)
    solution, residual = pl.pallas_call(
        last_kernel,
        compiler_params=PARAMS,
        out_shape=(flat, flat),
        in_specs=[SMEM] + [VMEM] * 9,
        out_specs=(HBM, HBM),
        scratch_shapes=[tall, close(wide, block_cols), close(wide, block_cols), pltpu.SemaphoreType.DMA((6,))],
    )(spot, *near(plane), *blocks, *vectors)
    return solution.T, residual.T


def solution(mesh):
    rows, cols = AXES[:2], AXES[2:]
    return jax.shard_map(
        body,
        mesh=Mesh(mesh.devices.reshape(Z, X, Y, K), AXES),
        in_specs=(P(rows, cols), P(cols, None), P(cols, None, None), P(cols)),
        out_specs=(P(cols, None), P(cols, None)),
        check_vma=False,
    )
```

```python
import jax
import jax.numpy as jnp
from jax import lax
from jax.experimental import pallas as pl
from jax.experimental.pallas import tpu as pltpu
from jax.sharding import Mesh, PartitionSpec as P


AXES = ("z", "x", "y", "k")
Z, X, Y, K = 8, 4, 4, 2
COLS = Y * K
TILE = 128
HALF = 144
LINES = 8
REACH = (3, 1, 0, 2)
STEPS = (2, 3, 1)


def place(z, x, y, k):
    return ((z % Z) * X + x % X) * COLS + (y % Y) * K + k % K


def everyone():
    return [(z, x, y, k) for z in range(Z) for x in range(X) for y in range(Y) for k in range(K)]


def moved(array, to):
    pairs = [(place(*at), place(*to(*at))) for at in everyone()]
    return lax.ppermute(array, AXES, pairs)


def other_core(array):
    return moved(array, lambda z, x, y, k: (z, x, y, k + 1))


def step_y(array, step):
    return moved(array, lambda z, x, y, k: (z, x, y + step, k))


def step_x(array, step):
    return moved(array, lambda z, x, y, k: (z, x + step, y, k))


def hop(plane, y, k):
    reach = REACH[(y - plane // K) % Y]
    return 1 + reach if k else -reach


def into_column(array):
    return moved(array, lambda z, x, y, k: (z + hop(z, y, k), x, z // K, z % K))


def parts_of(a):
    top = a.astype(jnp.bfloat16)
    rest = a - top.astype(jnp.float32)
    mid = rest.astype(jnp.bfloat16)
    return top, mid, (rest - mid.astype(jnp.float32)).astype(jnp.bfloat16)


def pass_of(a, b):
    return jnp.dot(a, b, preferred_element_type=jnp.float32)


def product(left, right):
    return product_of_parts(parts_of(left), right)


def product_of_parts(left_parts, right):
    n = right.shape[1]
    top, mid, low = left_parts
    side = jnp.concatenate(parts_of(right), axis=1)
    one = pass_of(top, side)
    two = pass_of(mid, side[:, : 2 * n])
    three = pass_of(low, side[:, :n])
    return one[:, :n] + ((one[:, n : 2 * n] + two[:, :n]) + ((one[:, 2 * n :] + two[:, n:]) + three))


def dot(a, b):
    return jnp.dot(a, b, precision=lax.Precision.HIGHEST, preferred_element_type=jnp.float32)


def summed(a):
    return jnp.sum(a, axis=0, keepdims=True)


def put_rows(value, line, packed_ref):
    packed_ref[0:HALF, :] = jnp.concatenate([value[:HALF], value[HALF:]], axis=1)
    packed_ref[HALF:, :] = jnp.broadcast_to(line, (LINES, line.shape[1]))


def take_rows(x, block_refs, out_ref):
    wide = out_ref.shape[1]
    for step, ref in zip((0,) + STEPS, block_refs):
        at = pl.multiple_of(lax.rem(x + X - step, X) * (2 * HALF), 8)
        block = ref[0:HALF, :]
        out_ref[pl.ds(at, HALF), :] = block[:, :wide]
        out_ref[pl.ds(at + HALF, HALF), :] = block[:, wide:]


def copies_of(sources, targets, sems):
    return [pltpu.make_async_copy(s, t, sems.at[i]) for i, (s, t) in enumerate(zip(sources, targets))]


def thirds(ref):
    return [ref.at[pl.ds(3 * i, 3)] for i in range(ref.shape[0] // 3)]


def first_kernel(order_hbm, flat_hbm, tile_hbm, matrix_hbm, packed_ref, right, precond, masked, matrix, order_ref, flat, tiles, in_sems):
    arrivals = copies_of([order_hbm, flat_hbm, *thirds(tile_hbm), matrix_hbm], [order_ref, flat, *thirds(tiles), matrix], in_sems)
    for copy in arrivals:
        copy.start()
    eye = lax.broadcasted_iota(jnp.int32, (TILE, TILE), 0) == lax.broadcasted_iota(jnp.int32, (TILE, TILE), 1)
    wide = flat.shape[0]
    spans = [slice(t * TILE, (t + 1) * TILE) for t in range(tiles.shape[0])]
    arrivals[0].wait()
    across = [jnp.broadcast_to(order_ref[t : t + 1, :].astype(jnp.float32), (TILE, TILE)) for t in range(len(spans))]
    diagonal = jnp.concatenate([jnp.where(eye, a, 0.0).astype(jnp.bfloat16) for a in across], axis=0)
    down = pass_of(diagonal, jnp.ones((TILE, TILE), jnp.bfloat16))
    for copy in arrivals[1:-1]:
        copy.wait()
    sides = [flat[:, span].T for span in spans]
    kept = [jnp.where(across[t] == down[span], tiles[t], 0.0) for t, span in enumerate(spans)]
    owns = [dot(tile, side) for tile, side in zip(kept, sides)]
    gamma = jnp.zeros((8, wide), jnp.float32)
    for side, own in zip(sides, owns):
        gamma = gamma + jnp.sum((side * own).reshape(TILE // 8, 8, wide), axis=0)
    gamma = summed(gamma)
    for t, span in enumerate(spans):
        masked[t] = kept[t]
        right[span, :] = sides[t]
        precond[span, :] = owns[t]
    arrivals[-1].wait()
    put_rows(product(matrix[...], precond[...]), jnp.concatenate([gamma, jnp.zeros_like(gamma)], axis=1), packed_ref)


def split_kernel(after_ref, masked_ref, matrix_ref, *out_refs):
    for value, refs in ((masked_ref[...], out_refs[:3]), (matrix_ref[...], out_refs[3:])):
        for ref, part in zip(refs, parts_of(value)):
            ref[...] = part


def second_kernel(spot_ref, a_ref, b_ref, c_ref, d_ref, precond_ref, top_ref, mid_ref, low_ref, matrix_top, matrix_mid, matrix_low, packed_ref, image, second):
    wide = image.shape[1]
    take_rows(spot_ref[0] // COLS % X, (a_ref, b_ref, c_ref, d_ref), image)
    spans = [slice(t * TILE, (t + 1) * TILE) for t in range(top_ref.shape[0])]
    images = [image[span, :] for span in spans]
    seconds = [product_of_parts((top_ref[t], mid_ref[t], low_ref[t]), images[t]) for t in range(len(spans))]
    for span, value in zip(spans, seconds):
        second[span, :] = value
    delta = summed(image[...] * precond_ref[...])
    gamma = jnp.where(spot_ref[0] % COLS == 0, a_ref[HALF : HALF + 1, :wide], 0.0)
    put_rows(product_of_parts((matrix_top[...], matrix_mid[...], matrix_low[...]), second[...]), jnp.concatenate([gamma, delta], axis=1), packed_ref)


def third_kernel(spot_ref, own_ref, right_ref, precond_ref, image_ref, second_ref, dots_ref):
    wide = right_ref.shape[1]
    gamma, delta = own_ref[HALF : HALF + 1, :wide], own_ref[HALF : HALF + 1, wide:]
    alpha = gamma / delta
    first = spot_ref[0] // COLS % X * (2 * HALF)
    total = [jnp.zeros((1, wide), jnp.float32)] * 2
    for part in range(2):
        rows = pl.ds(pl.multiple_of(first + part * HALF, 8), HALF)
        third = own_ref[0:HALF, part * wide : (part + 1) * wide]
        precond = precond_ref[rows, :] - alpha * second_ref[rows, :]
        residual = right_ref[rows, :] - alpha * image_ref[rows, :]
        image = image_ref[rows, :] - alpha * third
        total = [total[0] + summed(residual * precond), total[1] + summed(image * precond)]
    dots_ref[...] = jnp.concatenate(total, axis=1)


def last_kernel(spot_ref, dots_ref, a_ref, b_ref, c_ref, d_ref, right_ref, precond_ref, image_ref, second_ref, solution_hbm, residual_hbm, third, solution, residual, sems):
    wide = right_ref.shape[1]
    take_rows(spot_ref[0] // COLS % X, (a_ref, b_ref, c_ref, d_ref), third)
    gamma, delta = a_ref[HALF : HALF + 1, :wide], a_ref[HALF : HALF + 1, wide:]
    alpha = gamma / delta
    dots = jnp.sum(dots_ref[...], axis=0)
    gamma_next, delta_next = dots[:, :wide], dots[:, wide:]
    beta = gamma_next / gamma
    step = gamma_next / (delta_next - beta * gamma_next / alpha)
    kappa = alpha + (step + step * beta)
    cross = step * alpha
    count = right_ref.shape[0] // TILE
    leaving = []
    for t in range(count):
        rows = pl.ds(t * TILE, TILE)
        solution[:, rows] = (kappa * precond_ref[rows, :] - cross * second_ref[rows, :]).T
        residual[:, rows] = ((right_ref[rows, :] - kappa * image_ref[rows, :]) + cross * third[rows, :]).T
        if t % 3 == 2:
            done = pl.ds((t - 2) * TILE, 3 * TILE)
            for source, target in ((solution, solution_hbm), (residual, residual_hbm)):
                leaving.append(pltpu.make_async_copy(source.at[:, done], target.at[:, done], sems.at[len(leaving)]))
                leaving[-1].start()
    for copy in leaving:
        copy.wait()


def shaped(*dims):
    return jax.ShapeDtypeStruct(dims, jnp.float32)


def close(*dims):
    return pltpu.VMEM(dims, jnp.float32)


def near(*arrays):
    return [pltpu.with_memory_space_constraint(a, pltpu.VMEM) for a in arrays]


def far(*arrays):
    return [pltpu.with_memory_space_constraint(a, pltpu.HBM) for a in arrays]


PARAMS = pltpu.CompilerParams(vmem_limit_bytes=12 << 20)
SMEM = pl.BlockSpec(memory_space=pltpu.SMEM)
VMEM = pl.BlockSpec(memory_space=pltpu.VMEM)
HBM = pl.BlockSpec(memory_space=pltpu.HBM)


def added_over_col(array):
    both = array + other_core(array)
    around = [step_y(both, step) for step in STEPS]
    return both + around[0] + around[1] + around[2]


def spread_out(packed, *arrays):
    own = into_column(added_over_col(packed))
    return near(own, *[step_x(own, step) for step in STEPS]), near(*arrays)


def body(normal_matrix, right_side, tile_inverse, order_ids):
    block_rows, block_cols = normal_matrix.shape
    wide = right_side.shape[1]
    count = tile_inverse.shape[0]
    spot = lax.axis_index(AXES).astype(jnp.int32).reshape(1)
    square = close(count, TILE, TILE)
    tall = close(block_cols, wide)
    packed_shape = close(HALF + LINES, 2 * wide)

    packed, right, precond, masked, matrix = pl.pallas_call(
        first_kernel,
        compiler_params=PARAMS,
        out_shape=(packed_shape, tall, tall, square, close(block_rows, block_cols)),
        in_specs=[HBM] * 4,
        scratch_shapes=[pltpu.VMEM((count, TILE), jnp.int32), close(wide, block_cols), square, pltpu.SemaphoreType.DMA((6,))],
    )(*far(order_ids.reshape(count, TILE), right_side.T, tile_inverse, normal_matrix))
    blocks, (precond, masked, matrix) = spread_out(packed, precond, masked, matrix)
    split = pl.pallas_call(
        split_kernel,
        compiler_params=PARAMS,
        out_shape=[pltpu.VMEM(a.shape, jnp.bfloat16) for a in (masked,) * 3 + (matrix,) * 3],
        in_specs=[VMEM] * 3,
    )(blocks[0], masked, matrix)

    packed, image, second = pl.pallas_call(
        second_kernel,
        compiler_params=PARAMS,
        out_shape=(packed_shape, tall, tall),
        in_specs=[SMEM] + [VMEM] * 11,
    )(spot, *blocks, precond, *near(*split))
    blocks, vectors = spread_out(packed, right, precond, image, second)

    dots = pl.pallas_call(
        third_kernel,
        compiler_params=PARAMS,
        out_shape=close(1, 2 * wide),
        in_specs=[SMEM] + [VMEM] * 5,
    )(spot, blocks[0], *vectors)

    plane = jnp.broadcast_to(dots, (X * COLS, *dots.shape))
    plane = lax.all_to_all(plane, ("x", "y", "k"), 0, 0, tiled=True)
    flat = shaped(wide, block_cols)
    solution, residual = pl.pallas_call(
        last_kernel,
        compiler_params=PARAMS,
        out_shape=(flat, flat),
        in_specs=[SMEM] + [VMEM] * 9,
        out_specs=(HBM, HBM),
        scratch_shapes=[tall, close(wide, block_cols), close(wide, block_cols), pltpu.SemaphoreType.DMA((6,))],
    )(spot, *near(plane), *blocks, *vectors)
    return solution.T, residual.T


def solution(mesh):
    rows, cols = AXES[:2], AXES[2:]
    return jax.shard_map(
        body,
        mesh=Mesh(mesh.devices.reshape(Z, X, Y, K), AXES),
        in_specs=(P(rows, cols), P(cols, None), P(cols, None, None), P(cols)),
        out_specs=(P(cols, None), P(cols, None)),
        check_vma=False,
    )
```
